256 devices in a mesh: expert: 64 (over x, z, core), hidden: 4 (over y).
Axes of the slice: x: 4, y: 4, z: 8, core: 2. Of those that a mesh axis runs over, the one named last changes fastest.
Arguments:
- tokens: bfloat16 [1024, 7168], P('expert', 'hidden'), may hold values from -6 to 6
- routes: int32 [1024, 8], P('expert'), may hold values from 0 to 63, as said below
- combine: float32 [1024, 8], P('expert'), may hold values from 0.05 to 0.5
- w_gate: bfloat16 [64, 7168, 1024], P('expert', None, 'hidden'), may hold values from -0.0625 to 0.0625
- w_up: bfloat16 [64, 7168, 1024], P('expert', None, 'hidden'), may hold values from -0.0625 to 0.0625
- w_down: bfloat16 [64, 1024, 7168], P('expert', 'hidden'), may hold values from -0.1875 to 0.1875
- cotangent: bfloat16 [1024, 7168], P('expert', 'hidden'), may hold values from -6 to 6
Outputs:
- output: bfloat16 [1024, 7168], P('expert', 'hidden')
- grad_tokens: bfloat16 [1024, 7168], P('expert', 'hidden')
The draws below stay inside these ranges and needn't reach their ends.
Inputs may be any that keep to these rules, and one draw needn't show every extreme that they name: `routes`: each row names 8 different experts. In each aligned block of 16 rows (the rows of one device) no expert is named by more than 4 rows, and the same expert is named by exactly 4 rows in every block.
All inputs are finite; a program needn't handle non-finite values.
Results may differ from the reference program's by a relative error of at most 0.012.
Values may be sent and summed in bfloat16 or wider, within the bound.
No kernel may reach another device: no remote copies, remote signals or barrier semaphores. Data moves between devices by JAX's collectives and lax.ppermute only.
A program may use at most 128 MiB of HBM per device.

```python
import math
import jax
import jax.numpy as jnp
from jax import lax

D = 7168
FF = 1024
TOP = 8
TOK_DEV = 16
EXPERTS = 64
TOKENS = 1024
CAP = 4
N_EXPERT = 64
N_HIDDEN = 4


def draw_routes(key, part):
    blocks = TOKENS // TOK_DEV
    mean_load = TOK_DEV * TOP // EXPERTS
    pair_count = TOK_DEV * TOP
    half_count = (EXPERTS - 2) // 2
    hot_key, block_key = jax.random.split(jax.random.fold_in(key, 17))
    hot_expert = jax.random.randint(hot_key, (), 0, EXPERTS).astype(jnp.int32)
    positions = jnp.arange(pair_count, dtype=jnp.int32)

    def one_block(sub_key):
        order_key, shift_key, token_key = jax.random.split(sub_key, 3)
        others = jax.random.permutation(order_key, EXPERTS - 1).astype(jnp.int32)
        others = jnp.where(others >= hot_expert, others + 1, others)
        shifts = jax.random.randint(shift_key, (half_count,), 0, mean_load + 1).astype(jnp.int32)
        head_loads = jnp.array([2 * mean_load, 0], jnp.int32)
        loads = jnp.concatenate([head_loads, mean_load + shifts, mean_load - shifts])
        owners = jnp.concatenate([hot_expert[None], others])
        ends = jnp.cumsum(loads)
        run_index = jnp.sum((positions[:, None] >= ends[None, :]).astype(jnp.int32), axis=1)
        picks = owners[run_index].reshape(TOP, TOK_DEV).T
        return picks[jax.random.permutation(token_key, TOK_DEV)]
    block_keys = jax.random.split(block_key, blocks)
    return jax.vmap(one_block)(block_keys).reshape(TOKENS, TOP).astype(jnp.int32)


def block_levels(rng, extent, cuts, smallest, high):
    def one(dim, parts):
        draws = jax.random.uniform(jax.random.fold_in(jax.random.fold_in(rng, 6), dim), (parts,), jnp.float32, smallest / len(cuts), high / len(cuts))
        return jnp.repeat(jnp.exp(draws), extent[dim] // parts).reshape((-1,) + (1,) * (len(extent) - dim - 1))

    loudness = one(*cuts[0])
    for cut in cuts[1:]:
        loudness = loudness * one(*cut)
    return loudness


def normal_values(stream_key, shape, spread, limit, cuts=(), kind=jnp.bfloat16):
    drawn = jax.random.normal(stream_key, shape, jnp.float32) * spread
    if len(cuts) > 0:
        drawn = block_levels(stream_key, shape, cuts, -0.22, 0.18) * drawn
    return jnp.clip(drawn, min=-limit, max=limit).astype(kind)


def setup_inputs(seed: int = 0) -> dict:
    seeds = jax.random.split(jax.random.key(seed), 8)
    tokens = normal_values(seeds[0], (TOKENS, D), 1.0, 6.0, ((0, 64), (1, 4)))
    routes = draw_routes(jax.random.fold_in(seeds[7], 71), 0)
    combine = jnp.clip(jnp.exp(math.log(0.5) - 2.3025851 * jax.random.uniform(seeds[2], (TOKENS, TOP), jnp.float32) ** block_levels(seeds[2], (TOKENS, TOP), ((0, 64),), -0.2, 0.2)), 0.05, 0.5)
    w_gate = normal_values(seeds[3], (EXPERTS, D, FF), D ** -0.5, 0.0625, ((0, 64), (2, 4)))
    w_up = normal_values(seeds[4], (EXPERTS, D, FF), D ** -0.5, 0.0625, ((0, 64), (2, 4)))
    w_down = normal_values(seeds[5], (EXPERTS, FF, D), FF ** -0.5, 0.1875, ((0, 64), (1, 4)))
    cotangent = normal_values(seeds[6], (TOKENS, D), 1.0, 6.0, ((0, 64), (1, 4)))
    return {"tokens": tokens, "routes": routes, "combine": combine, "w_gate": w_gate, "w_up": w_up, "w_down": w_down, "cotangent": cotangent}


def expert_pass(rows_in, grads_in, gate_weight, up_weight, down_weight):
    gate_pre = jnp.dot(rows_in, gate_weight, preferred_element_type=jnp.float32)
    up_pre = jnp.dot(rows_in, up_weight, preferred_element_type=jnp.float32)
    sigmoid_gate = jax.nn.sigmoid(gate_pre)
    activated = gate_pre * sigmoid_gate
    hidden_act = (activated * up_pre).astype(jnp.bfloat16)
    back_hidden = jnp.dot(grads_in, down_weight.T, preferred_element_type=jnp.float32)
    grad_gate = (back_hidden * up_pre * sigmoid_gate * (1.0 + gate_pre * (1.0 - sigmoid_gate))).astype(jnp.bfloat16)
    grad_up = (back_hidden * activated).astype(jnp.bfloat16)
    quarter_units = FF // N_HIDDEN
    out_total = jnp.zeros((rows_in.shape[0], D), jnp.float32)
    grad_total = jnp.zeros((rows_in.shape[0], D), jnp.float32)
    for quarter in range(N_HIDDEN):
        lower = quarter * quarter_units
        upper = lower + quarter_units
        out_part = jnp.dot(hidden_act[:, lower:upper], down_weight[lower:upper], preferred_element_type=jnp.float32)
        out_part = lax.optimization_barrier(out_part.astype(jnp.bfloat16))
        out_total = out_total + out_part.astype(jnp.float32)
        grad_part = jnp.dot(grad_gate[:, lower:upper], gate_weight[:, lower:upper].T, preferred_element_type=jnp.float32)
        grad_part = grad_part + jnp.dot(grad_up[:, lower:upper], up_weight[:, lower:upper].T, preferred_element_type=jnp.float32)
        grad_part = lax.optimization_barrier(grad_part.astype(jnp.bfloat16))
        grad_total = grad_total + grad_part.astype(jnp.float32)
    return out_total.astype(jnp.bfloat16), grad_total.astype(jnp.bfloat16)


def reference(tokens, routes, combine, w_gate, w_up, w_down, cotangent):
    pair_count = TOKENS * TOP
    flat_routes = routes.reshape(pair_count).astype(jnp.int32)
    order = jnp.argsort(flat_routes, stable=True).astype(jnp.int32)
    expert_ids = jnp.arange(EXPERTS, dtype=jnp.int32)
    counts = jnp.sum((flat_routes[None, :] == expert_ids[:, None]).astype(jnp.int32), axis=1).astype(jnp.int32)
    starts = (jnp.cumsum(counts) - counts).astype(jnp.int32)
    buffer_rows = N_EXPERT * CAP
    padded_order = jnp.concatenate([order, jnp.zeros((buffer_rows,), jnp.int32)])
    flat_combine = combine.reshape(pair_count)

    def per_expert(totals, expert):
        out_total, grad_total = totals
        chosen = lax.dynamic_slice_in_dim(padded_order, starts[expert], buffer_rows)
        live = jnp.arange(buffer_rows, dtype=jnp.int32) < counts[expert]
        token_index = (chosen // TOP).astype(jnp.int32)
        scale = jnp.where(live, flat_combine[chosen], jnp.zeros((buffer_rows,), jnp.float32))
        out_rows, grad_rows = expert_pass(tokens[token_index], cotangent[token_index], w_gate[expert], w_up[expert], w_down[expert])
        out_total = out_total.at[token_index].add(scale[:, None] * out_rows.astype(jnp.float32))
        grad_total = grad_total.at[token_index].add(scale[:, None] * grad_rows.astype(jnp.float32))
        return (out_total, grad_total), None

    zero_total = jnp.zeros((TOKENS, D), jnp.float32)
    (out_total, grad_total), _ = lax.scan(per_expert, (zero_total, zero_total), expert_ids)
    return out_total.astype(jnp.bfloat16), grad_total.astype(jnp.bfloat16)
```

```python
import jax
import jax.numpy as jnp
from jax import lax
from jax.experimental import pallas as pl
from jax.experimental.pallas import tpu as pltpu
from jax.sharding import PartitionSpec as P

CHUNKS = 2


def gates_kernel(width, sums_ref, out_ref):
    rows = sums_ref.shape[0]
    gate = sums_ref[:, 0:width]
    up = sums_ref[:, width : 2 * width]
    back = pltpu.roll(sums_ref[:, 2 * width : 3 * width], rows - 4, 0)
    first = lax.broadcasted_iota(jnp.int32, (rows, width), 0) % 8 < 4
    sig = jax.nn.sigmoid(gate)
    act = gate * sig
    zero = jnp.zeros_like(act)
    hidden = act * up
    grad_gate = back * up * sig * (1.0 + gate * (1.0 - sig))
    grad_up = back * act
    out_ref[:, 0:width] = jnp.where(first, zero, pltpu.roll(grad_gate, 4, 0)).astype(jnp.bfloat16)
    out_ref[:, width : 2 * width] = jnp.where(first, zero, pltpu.roll(grad_up, 4, 0)).astype(
        jnp.bfloat16
    )
    out_ref[:, 2 * width : 3 * width] = jnp.where(first, hidden, zero).astype(jnp.bfloat16)


def gates(sums):
    rows, cols = sums.shape
    block = 128
    return pl.pallas_call(
        lambda a, b: gates_kernel(cols // 3, a, b),
        grid=(rows // block,),
        in_specs=[pl.BlockSpec((block, cols), lambda i: (i, 0))],
        out_specs=pl.BlockSpec((block, cols), lambda i: (i, 0)),
        out_shape=jax.ShapeDtypeStruct((rows, cols), jnp.bfloat16),
        name="gates",
    )(sums)


def per_device(tokens, routes, combine, w_gate, w_up, w_down, cotangent):
    toks, slice_cols = tokens.shape
    sources = lax.axis_size("expert")
    parts = lax.axis_size("hidden")
    cap = 4
    group = 2 * cap
    rows = sources * group
    half = rows // 2
    chunk = slice_cols // CHUNKS
    me = lax.axis_index("hidden")

    right = [(i, (i + 1) % parts) for i in range(parts)]
    left = [(i, (i - 1) % parts) for i in range(parts)]

    def to_right(v):
        return lax.ppermute(v, "hidden", right)

    def to_left(v):
        return lax.ppermute(v, "hidden", left)

    def exchange(v):
        out = lax.all_to_all(
            v.reshape(sources, group, v.shape[1]), "expert", split_axis=0, concat_axis=0, tiled=True
        )
        return out.reshape(rows, v.shape[1])

    row = lax.broadcasted_iota(jnp.int32, (toks, rows), 1)
    owner = row // group
    hit = routes[:, :, None] == owner[:, None, :]
    named = jnp.any(hit, axis=1)
    weight = jnp.sum(jnp.where(hit, combine[:, :, None], 0.0), axis=1)
    earlier = (
        lax.broadcasted_iota(jnp.int32, (toks, toks), 0)
        > lax.broadcasted_iota(jnp.int32, (toks, toks), 1)
    ).astype(jnp.bfloat16)
    rank = jnp.dot(earlier, named.astype(jnp.bfloat16), preferred_element_type=jnp.float32)
    placed = named & (rank.astype(jnp.int32) == row % cap)
    is_token = row % group < cap
    choose = jnp.concatenate([placed & is_token, placed & ~is_token], axis=0)
    select = choose.astype(jnp.bfloat16)
    table = jnp.concatenate([tokens, cotangent], axis=0)

    def pack(j):
        return lax.dot_general(
            select,
            table[:, j * chunk : (j + 1) * chunk],
            (((0,), (0,)), ((), ())),
            preferred_element_type=jnp.float32,
        ).astype(jnp.bfloat16)

    def rel(k):
        start = ((me + k) % parts) * slice_cols
        return jnp.concatenate(
            [
                lax.dynamic_slice_in_dim(w_gate, start, slice_cols, 0),
                lax.dynamic_slice_in_dim(w_up, start, slice_cols, 0),
                lax.dynamic_slice_in_dim(w_down, start, slice_cols, 1).T,
            ],
            axis=1,
        )

    w_gate, w_up, w_down = w_gate[0], w_up[0], w_down[0]
    weights = [rel(k) for k in range(parts)]

    sums = None
    previous = None
    for j in range(CHUNKS):
        packed = pack(j)
        if previous is not None:
            packed, previous = lax.optimization_barrier((packed, previous))
        own = exchange(packed)
        previous = own
        top, bottom = own[:half], own[half:]
        l_top = to_right(top)
        r_bottom = to_left(bottom)
        l_bottom = to_right(bottom)
        r_top = to_left(top)
        o_top = to_right(l_top)
        o_bottom = to_left(r_bottom)
        cols = slice(j * chunk, (j + 1) * chunk)
        for k, v in (
            (0, own),
            (3, jnp.concatenate([l_top, l_bottom], axis=0)),
            (1, jnp.concatenate([r_top, r_bottom], axis=0)),
            (2, jnp.concatenate([o_top, o_bottom], axis=0)),
        ):
            term = jnp.dot(v, weights[k][cols], preferred_element_type=jnp.float32)
            sums = term if sums is None else sums + term

    grads = gates(sums)
    width = w_gate.shape[1]

    def product(k, j, lo, hi):
        w = weights[k][j * chunk : (j + 1) * chunk]
        w = jnp.concatenate([w[:, : 2 * width], w[:, 2 * width :]], axis=1)
        return lax.dot_general(
            grads[lo:hi], w, (((1,), (1,)), ((), ())), preferred_element_type=jnp.float32
        )

    spread = choose * jnp.concatenate([weight, weight], axis=0)
    coarse = lax.reduce_precision(spread, 8, 7)
    fine = (spread - coarse).astype(jnp.bfloat16)
    coarse = coarse.astype(jnp.bfloat16)

    results = []
    for j in range(CHUNKS):
        o_top = to_right(product(2, j, 0, half).astype(jnp.bfloat16))
        o_bottom = to_left(product(2, j, half, rows).astype(jnp.bfloat16))
        l_bottom = to_right(product(1, j, half, rows).astype(jnp.bfloat16))
        r_top = to_left(product(3, j, 0, half).astype(jnp.bfloat16))
        l_top = to_right((product(1, j, 0, half) + o_top.astype(jnp.float32)).astype(jnp.bfloat16))
        r_bottom = to_left(
            (product(3, j, half, rows) + o_bottom.astype(jnp.float32)).astype(jnp.bfloat16)
        )
        mine = product(0, j, 0, rows)
        total = (
            mine
            + jnp.concatenate([l_top, l_bottom], axis=0).astype(jnp.float32)
            + jnp.concatenate([r_top, r_bottom], axis=0).astype(jnp.float32)
        ).astype(jnp.bfloat16)
        back = exchange(total)
        mixed = jnp.dot(coarse, back, preferred_element_type=jnp.float32) + jnp.dot(
            fine, back, preferred_element_type=jnp.float32
        )
        results.append(mixed.astype(jnp.bfloat16))
    result = jnp.concatenate(results, axis=1)
    return result[:toks], result[toks:]


def solution(mesh):
    return jax.shard_map(
        per_device,
        mesh=mesh,
        in_specs=(
            P("expert", "hidden"),
            P("expert", None),
            P("expert", None),
            P("expert", None, "hidden"),
            P("expert", None, "hidden"),
            P("expert", "hidden", None),
            P("expert", "hidden"),
        ),
        out_specs=(P("expert", "hidden"), P("expert", "hidden")),
        check_vma=False,
    )
```

```python
import jax
import jax.numpy as jnp
from jax import lax
from jax.experimental import pallas as pl
from jax.experimental.pallas import tpu as pltpu
from jax.sharding import PartitionSpec as P


DIRECT = 384
CAP = 4


def gates_kernel(sums_ref, x_ref, far_ref, *refs):
    near_refs, (out_ref, relay_ref) = refs[:-2], refs[-2:]
    rows, cols = sums_ref.shape
    width = cols // 3
    depth = near_refs[0].shape[0]
    sums = sums_ref[...]
    for k, w_ref in enumerate(near_refs):
        x = x_ref[:, k * depth : (k + 1) * depth]
        sums = sums + jnp.dot(x, w_ref[...], preferred_element_type=jnp.float32)
    gate = sums[:, 0:width]
    up = sums[:, width : 2 * width]
    back = pltpu.roll(sums[:, 2 * width : 3 * width], rows - CAP, 0)
    first = lax.broadcasted_iota(jnp.int32, (rows, width), 0) % (2 * CAP) < CAP
    sig = jax.nn.sigmoid(gate)
    act = gate * sig
    zero = jnp.zeros_like(act)
    hidden = act * up
    grad_gate = back * up * sig * (1.0 + gate * (1.0 - sig))
    grad_up = back * act
    out = jnp.concatenate(
        [
            jnp.where(first, zero, pltpu.roll(grad_gate, CAP, 0)),
            jnp.where(first, zero, pltpu.roll(grad_up, CAP, 0)),
            jnp.where(first, hidden, zero),
        ],
        axis=1,
    ).astype(jnp.bfloat16)
    out_ref[...] = out
    relay_ref[...] = lax.dot_general(
        out, far_ref[...], (((1,), (1,)), ((), ())), preferred_element_type=jnp.float32
    ).astype(jnp.bfloat16)


def gates(sums, x, far, near):
    rows, cols = sums.shape
    depth = x.shape[1]
    reach = far.shape[0]
    block = 128
    return pl.pallas_call(
        gates_kernel,
        grid=(rows // block,),
        in_specs=[
            pl.BlockSpec((block, cols), lambda i: (i, 0)),
            pl.BlockSpec((block, depth), lambda i: (i, 0)),
            pl.BlockSpec(far.shape, lambda i: (0, 0)),
        ]
        + [pl.BlockSpec(w.shape, lambda i: (0, 0)) for w in near],
        out_specs=(
            pl.BlockSpec((block, cols), lambda i: (i, 0)),
            pl.BlockSpec((block, reach), lambda i: (i, 0)),
        ),
        out_shape=(
            jax.ShapeDtypeStruct((rows, cols), jnp.bfloat16),
            jax.ShapeDtypeStruct((rows, reach), jnp.bfloat16),
        ),
        cost_estimate=pl.CostEstimate(
            flops=2 * rows * cols * (depth + reach),
            bytes_accessed=rows * (cols * 6 + depth * 2 + reach * 2) + (depth + reach) * cols * 2,
            transcendentals=rows * cols // 3,
        ),
        name="gates",
    )(sums, x, far, *near)


def per_device(tokens, routes, combine, w_gate, w_up, w_down, cotangent):
    toks, slice_cols = tokens.shape
    sources = lax.axis_size("expert")
    parts = lax.axis_size("hidden")
    group = 2 * CAP
    rows = sources * group
    half = rows // 2
    me = lax.axis_index("hidden")
    f32, bf16 = jnp.float32, jnp.bfloat16

    def shift(v, k):
        return lax.ppermute(v, "hidden", [(i, (i + k) % parts) for i in range(parts)])

    def exchange(v):
        out = lax.all_to_all(
            v.reshape(sources, group, v.shape[1]), "expert", split_axis=0, concat_axis=0, tiled=True
        )
        return out.reshape(rows, v.shape[1])

    table = jnp.concatenate([tokens, cotangent], axis=0)
    direct = table[:, :DIRECT]
    direct_parts = [direct] + [shift(direct, parts - k) for k in range(1, parts)]

    row = lax.broadcasted_iota(jnp.int32, (toks, rows), 1)
    owner = row // group
    hit = routes[:, :, None] == owner[:, None, :]
    named = jnp.any(hit, axis=1)
    weight = jnp.sum(jnp.where(hit, combine[:, :, None], 0.0), axis=1)
    earlier = (
        lax.broadcasted_iota(jnp.int32, (toks, toks), 0)
        > lax.broadcasted_iota(jnp.int32, (toks, toks), 1)
    ).astype(bf16)
    rank = jnp.dot(earlier, named.astype(bf16), preferred_element_type=f32)
    placed = named & (rank.astype(jnp.int32) == row % CAP)
    is_token = row % group < CAP
    choose = jnp.concatenate([placed & is_token, placed & ~is_token], axis=0)
    select = choose.astype(bf16)

    def pack(values):
        return lax.dot_general(
            select, values, (((0,), (0,)), ((), ())), preferred_element_type=f32
        ).astype(bf16)

    w_gate, w_up, w_down = w_gate[0], w_up[0], w_down[0]

    def relative(k, lo, hi):
        start = ((me + k) % parts) * slice_cols + lo
        return jnp.concatenate(
            [
                lax.dynamic_slice_in_dim(w_gate, start, hi - lo, 0),
                lax.dynamic_slice_in_dim(w_up, start, hi - lo, 0),
                lax.dynamic_slice_in_dim(w_down, start, hi - lo, 1).T,
            ],
            axis=1,
        )

    w_near = [relative(k, 0, DIRECT) for k in range(parts)]
    w_far = [relative(k, DIRECT, slice_cols) for k in range(parts)]

    own = exchange(pack(table[:, DIRECT:]))
    packed_direct = pack(jnp.concatenate(direct_parts, axis=1))
    own, packed_direct, w_near, w_far = lax.optimization_barrier(
        (own, packed_direct, w_near, w_far)
    )
    top, bottom = own[:half], own[half:]
    l_top = shift(top, 1)
    r_bottom = shift(bottom, -1)
    arrived_direct = exchange(packed_direct)
    top, bottom, l_top, r_bottom = lax.optimization_barrier((top, bottom, l_top, r_bottom))
    o_top = shift(l_top, 1)
    o_bottom = shift(r_bottom, -1)
    l_bottom = shift(bottom, 1)
    r_top = shift(top, -1)
    sums = jnp.dot(own, w_far[0], preferred_element_type=f32)
    for k, v in (
        (2, jnp.concatenate([o_top, o_bottom], axis=0)),
        (3, jnp.concatenate([l_top, l_bottom], axis=0)),
        (1, jnp.concatenate([r_top, r_bottom], axis=0)),
    ):
        sums = sums + jnp.dot(v, w_far[k], preferred_element_type=f32)
    grads, relay = gates(sums, arrived_direct, w_far[2], w_near)

    def product(w, lo, hi):
        return lax.dot_general(
            grads[lo:hi], w, (((1,), (1,)), ((), ())), preferred_element_type=f32
        )

    spread = choose * jnp.concatenate([weight, weight], axis=0)
    coarse = lax.reduce_precision(spread, 8, 7)
    fine = (spread - coarse).astype(bf16)
    coarse = coarse.astype(bf16)

    def mix(back):
        return jnp.dot(coarse, back, preferred_element_type=f32) + jnp.dot(
            fine, back, preferred_element_type=f32
        )

    o_top = shift(relay[:half], 1)
    o_bottom = shift(relay[half:], -1)
    back_direct = exchange(
        jnp.concatenate([product(w, 0, rows) for w in w_near], axis=1).astype(bf16)
    )
    p_bottom = product(w_far[1], half, rows).astype(bf16)
    p_top = product(w_far[3], 0, half).astype(bf16)
    o_top, o_bottom, p_bottom, p_top = lax.optimization_barrier((o_top, o_bottom, p_bottom, p_top))
    l_top = shift((product(w_far[1], 0, half) + o_top.astype(f32)).astype(bf16), 1)
    r_bottom = shift((product(w_far[3], half, rows) + o_bottom.astype(f32)).astype(bf16), -1)
    l_bottom = shift(p_bottom, 1)
    r_top = shift(p_top, -1)
    total = (
        product(w_far[0], 0, rows)
        + jnp.concatenate([l_top, l_bottom], axis=0).astype(f32)
        + jnp.concatenate([r_top, r_bottom], axis=0).astype(f32)
    ).astype(bf16)
    total, back_direct = lax.optimization_barrier((total, back_direct))
    back_far = exchange(total)

    mixed = mix(back_direct)
    near = mixed[:, :DIRECT]
    for k in range(1, parts):
        near = near + shift(mixed[:, k * DIRECT : (k + 1) * DIRECT].astype(bf16), k).astype(f32)
    result = jnp.concatenate([near.astype(bf16), mix(back_far).astype(bf16)], axis=1)
    return result[:toks], result[toks:]


def solution(mesh):
    return jax.shard_map(
        per_device,
        mesh=mesh,
        in_specs=(
            P("expert", "hidden"),
            P("expert", None),
            P("expert", None),
            P("expert", None, "hidden"),
            P("expert", None, "hidden"),
            P("expert", "hidden", None),
            P("expert", "hidden"),
        ),
        out_specs=(P("expert", "hidden"), P("expert", "hidden")),
        check_vma=False,
    )
```

```python
import jax
import jax.numpy as jnp
from jax import lax
from jax.experimental import pallas as pl
from jax.experimental.pallas import tpu as pltpu
from jax.sharding import PartitionSpec as P


DIRECT = 384
CAP = 4
LANES = 128
MIB = 1 << 20
F32, BF16 = jnp.float32, jnp.bfloat16
ANY = pl.BlockSpec(memory_space=pl.ANY)
HBM = pl.BlockSpec(memory_space=pltpu.HBM)
SMEM = pl.BlockSpec(memory_space=pltpu.SMEM)
VMEM = pl.BlockSpec(memory_space=pltpu.VMEM)


def dot(a, b):
    return jnp.dot(a, b, preferred_element_type=F32)


def dot_t(a, b):
    return lax.dot_general(a, b, (((1,), (1,)), ((), ())), preferred_element_type=F32)


class Plan:
    def __init__(self, parts, depth, width):
        self.parts, self.depth, self.width = parts, depth, width
        self.slice = depth // parts
        self.far = self.slice - DIRECT

    def weight_scratch(self, reach):
        w = self.width
        return [pltpu.VMEM((reach, w), BF16), pltpu.VMEM((reach, w), BF16), pltpu.VMEM((w, reach), BF16)]

    def copies(self, me_ref, k, lo, reach, hbm, bufs, sems, at=0):
        start = pl.multiple_of(((me_ref[0] + k) % self.parts) * self.slice + lo, LANES)
        here, there = pl.ds(at, reach), pl.ds(start, reach)
        return [
            pltpu.make_async_copy(hbm[0].at[there, :], bufs[0].at[here, :], sems.at[0]),
            pltpu.make_async_copy(hbm[1].at[there, :], bufs[1].at[here, :], sems.at[1]),
            pltpu.make_async_copy(hbm[2].at[:, there], bufs[2].at[:, here], sems.at[2]),
        ]


def run(copies):
    for c in copies:
        c.start()
    return copies


def done(copies):
    for c in copies:
        c.wait()


def forward(x, bufs):
    return dot(x, bufs[0][...]), dot(x, bufs[1][...]), dot_t(x, bufs[2][...])


def backward(h, bufs, width):
    return (
        dot_t(h[:, :width], bufs[0][...])
        + dot_t(h[:, width : 2 * width], bufs[1][...])
        + dot(h[:, 2 * width :], bufs[2][...])
    )


def call(kernel, outs, args, scratch, specs, flops, limit):
    moved = sum(a.size * a.dtype.itemsize for a, s in zip(args, specs) if s is VMEM)
    return pl.pallas_call(
        kernel,
        in_specs=specs,
        out_specs=[VMEM] * len(outs),
        out_shape=[jax.ShapeDtypeStruct(s, t) for s, t in outs],
        scratch_shapes=scratch,
        compiler_params=pltpu.CompilerParams(vmem_limit_bytes=limit * MIB),
        cost_estimate=pl.CostEstimate(flops=flops, bytes_accessed=moved + 4 * MIB, transcendentals=0),
    )(*args)


def partial_sums(plan, me, sources, sums, weights, limit):
    w = plan.width
    xs = [x for _, pieces in sources for x in pieces]
    rows = sum(x.shape[0] for x in sources[0][1])
    base = [] if sums is None else [sums]

    def kernel(me_ref, *refs):
        base_refs, x_refs = refs[: len(base)], list(refs[len(base) : len(base) + len(xs)])
        wg, wu, wd, out_ref = refs[len(base) + len(xs) : len(base) + len(xs) + 4]
        bufs, sems = refs[len(base) + len(xs) + 4 : -1], refs[-1]
        loads = [
            run(plan.copies(me_ref, k, DIRECT, plan.far, (wg, wu, wd), bufs[3 * i : 3 * i + 3], sems.at[i]))
            for i, (k, _) in enumerate(sources)
        ]
        for i, (_, pieces) in enumerate(sources):
            done(loads[i])
            first = 0
            for _ in pieces:
                x = x_refs.pop(0)
                last = first + x.shape[0]
                for t, term in enumerate(forward(x[...], bufs[3 * i : 3 * i + 3])):
                    cols = slice(t * w, (t + 1) * w)
                    if i > 0:
                        term = term + out_ref[first:last, cols]
                    elif base_refs:
                        term = term + base_refs[0][first:last, cols]
                    out_ref[first:last, cols] = term
                first = last

    return call(
        kernel,
        [((rows, 3 * w), F32)],
        (me, *base, *xs, *weights),
        plan.weight_scratch(plan.far) * len(sources) + [pltpu.SemaphoreType.DMA((len(sources), 3))],
        [SMEM] + [VMEM] * (len(base) + len(xs)) + [HBM] * 3,
        2 * rows * 3 * w * plan.far * len(sources),
        limit,
    )[0]


def gates(plan, me, sums, arrived, direct, weights):
    rows, w = sums.shape[0], plan.width
    half, block = rows // 2, 128
    order = (2,)
    n = len(order)
    near_cols = plan.parts * DIRECT

    def kernel(me_ref, sums_hbm, *refs):
        x_hbm, (direct_hbm, wg, wu, wd, out_ref, top_ref, bottom_ref, near_ref), rest = (
            refs[: 2 * n],
            refs[2 * n : 2 * n + 8],
            refs[2 * n + 8 :],
        )
        acc, x_buf, direct_buf = rest[:3]
        near, far, (n_sems, f_sems, x_sems, m_sems) = rest[3:6], rest[6:-4], rest[-4:]
        hbm = (wg, wu, wd)
        first_load = pltpu.make_async_copy(sums_hbm, acc, m_sems.at[0])
        first_load.start()
        loads = []
        for i, k in enumerate(order):
            weight_loads = run(plan.copies(me_ref, k, DIRECT, plan.far, hbm, far[3 * i : 3 * i + 3], f_sems.at[i]))
            x_loads = run(
                [pltpu.make_async_copy(x_hbm[2 * i + j], x_buf.at[2 * i + j], x_sems.at[2 * i + j]) for j in range(2)]
            )
            loads.append(weight_loads + x_loads)
        near_loads = [
            c
            for k in range(plan.parts)
            for c in run(plan.copies(me_ref, k, 0, DIRECT, hbm, near, n_sems.at[k], k * DIRECT))
        ]
        direct_load = pltpu.make_async_copy(direct_hbm, direct_buf, m_sems.at[1])
        direct_load.start()
        first_load.wait()
        for i in range(n):
            done(loads[i])
            for j in range(2):
                for t, term in enumerate(forward(x_buf[2 * i + j], far[3 * i : 3 * i + 3])):
                    acc[j * half : (j + 1) * half, t * w : (t + 1) * w] += term
        done(near_loads)
        direct_load.wait()
        for t, term in enumerate(forward(direct_buf[...], near)):
            acc[:, t * w : (t + 1) * w] += term

        @pl.loop(0, rows // block)
        def _(b):
            r = pl.ds(pl.multiple_of(b * block, block), block)
            gate, up = acc[r, 0:w], acc[r, w : 2 * w]
            back = pltpu.roll(acc[r, 2 * w : 3 * w], block - CAP, 0)
            first = lax.broadcasted_iota(jnp.int32, (block, w), 0) % (2 * CAP) < CAP
            sig = jax.nn.sigmoid(gate)
            act = gate * sig
            zero = jnp.zeros_like(act)
            grad_gate = back * up * sig * (1.0 + gate * (1.0 - sig))
            grad_up = back * act
            out_ref[r, 0:w] = jnp.where(first, zero, pltpu.roll(grad_gate, CAP, 0)).astype(BF16)
            out_ref[r, w : 2 * w] = jnp.where(first, zero, pltpu.roll(grad_up, CAP, 0)).astype(BF16)
            out_ref[r, 2 * w : 3 * w] = jnp.where(first, act * up, zero).astype(BF16)

        relay = backward(out_ref[...], far[-3:], w).astype(BF16)
        top_ref[...] = relay[:half]
        bottom_ref[...] = relay[half:]
        near_ref[...] = backward(out_ref[...], near, w).astype(BF16)

    scratch = [
        pltpu.VMEM((rows, 3 * w), F32),
        pltpu.VMEM((2 * n, half, plan.far), BF16),
        pltpu.VMEM((rows, near_cols), BF16),
        *plan.weight_scratch(near_cols),
        *(plan.weight_scratch(plan.far) * n),
        pltpu.SemaphoreType.DMA((plan.parts, 3)),
        pltpu.SemaphoreType.DMA((n, 3)),
        pltpu.SemaphoreType.DMA((2 * n,)),
        pltpu.SemaphoreType.DMA((2,)),
    ]
    return call(
        kernel,
        [
            ((rows, 3 * w), BF16),
            ((half, plan.far), BF16),
            ((half, plan.far), BF16),
            ((rows, near_cols), BF16),
        ],
        (me, sums, *arrived, direct, *weights),
        scratch,
        [SMEM] + [ANY] * (2 * n + 2) + [HBM] * 3,
        2 * rows * 3 * w * ((n + 1) * plan.far + 2 * near_cols),
        26,
    )


def products(plan, me, h, wanted, weights):
    w = plan.width
    reach = plan.far
    adds = [a for *_, a in wanted if a is not None]
    outs = [((last - first, reach), BF16) for _, first, last, _ in wanted]

    def kernel(me_ref, h_ref, *refs):
        add_refs = list(refs[: len(adds)])
        wg, wu, wd = refs[len(adds) : len(adds) + 3]
        out_refs = refs[len(adds) + 3 : len(adds) + 3 + len(outs)]
        bufs, sems = refs[len(adds) + 3 + len(outs) : -1], refs[-1]
        loads = [
            run(plan.copies(me_ref, k, DIRECT, reach, (wg, wu, wd), bufs[3 * i : 3 * i + 3], sems.at[i]))
            for i, (k, *_) in enumerate(wanted)
        ]
        for i, (_, first, last, extra) in enumerate(wanted):
            done(loads[i])
            value = backward(h_ref[first:last, :], bufs[3 * i : 3 * i + 3], w)
            if extra is not None:
                value = value + add_refs.pop(0)[...].astype(F32)
            out_refs[i][...] = value.astype(BF16)

    return call(
        kernel,
        outs,
        (me, h, *adds, *weights),
        plan.weight_scratch(reach) * len(wanted) + [pltpu.SemaphoreType.DMA((len(wanted), 3))],
        [SMEM] + [VMEM] * (1 + len(adds)) + [HBM] * 3,
        sum(2 * (last - first) * 3 * w * reach for _, first, last, _ in wanted),
        16,
    )


def per_device(tokens, routes, combine, w_gate, w_up, w_down, cotangent):
    toks, _ = tokens.shape
    sources = lax.axis_size("expert")
    parts = lax.axis_size("hidden")
    group = 2 * CAP
    rows = sources * group
    half = rows // 2
    plan = Plan(parts, w_gate.shape[1], w_gate.shape[2])
    me = lax.axis_index("hidden").astype(jnp.int32).reshape(1)
    weights = tuple(pltpu.with_memory_space_constraint(w[0], pltpu.HBM) for w in (w_gate, w_up, w_down))

    def shift(v, k):
        return lax.ppermute(v, "hidden", [(i, (i + k) % parts) for i in range(parts)])

    def exchange(v):
        out = lax.all_to_all(
            v.reshape(sources, group, v.shape[1]), "expert", split_axis=0, concat_axis=0, tiled=True
        )
        return out.reshape(rows, v.shape[1])

    table = jnp.concatenate([tokens, cotangent], axis=0)
    direct = table[:, :DIRECT]
    direct_parts = [direct] + [shift(direct, parts - k) for k in range(1, parts)]

    row = lax.broadcasted_iota(jnp.int32, (toks, rows), 1)
    owner = row // group
    hit = routes[:, :, None] == owner[:, None, :]
    named = jnp.any(hit, axis=1)
    weight = jnp.sum(jnp.where(hit, combine[:, :, None], 0.0), axis=1)
    earlier = (
        lax.broadcasted_iota(jnp.int32, (toks, toks), 0)
        > lax.broadcasted_iota(jnp.int32, (toks, toks), 1)
    ).astype(BF16)
    rank = dot(earlier, named.astype(BF16))
    placed = named & (rank.astype(jnp.int32) == row % CAP)
    is_token = row % group < CAP
    choose = jnp.concatenate([placed & is_token, placed & ~is_token], axis=0)
    select = choose.astype(BF16)

    def pack(values):
        return lax.dot_general(
            select, values, (((0,), (0,)), ((), ())), preferred_element_type=F32
        ).astype(BF16)

    own = exchange(pack(table[:, DIRECT:]))
    packed_direct = pack(jnp.concatenate(direct_parts, axis=1))
    own, packed_direct = lax.optimization_barrier((own, packed_direct))
    top, bottom = own[:half], own[half:]
    l_top = shift(top, 1)
    r_bottom = shift(bottom, -1)
    arrived_direct = exchange(packed_direct)
    l_bottom = shift(bottom, 1)
    r_top = shift(top, -1)
    o_top = shift(l_top, 1)
    o_bottom = shift(r_bottom, -1)
    sums = partial_sums(plan, me, [(0, [own])], None, weights, 14)
    sums = partial_sums(plan, me, [(3, [l_top, l_bottom]), (1, [r_top, r_bottom])], sums, weights, 18)
    grads, relay_top, relay_bottom, near = gates(plan, me, sums, (o_top, o_bottom), arrived_direct, weights)

    o_top = shift(relay_top, 1)
    o_bottom = shift(relay_bottom, -1)
    back_direct = exchange(near)
    p_bottom, p_top = products(plan, me, grads, [(1, half, rows, None), (3, 0, half, None)], weights)
    l_bottom = shift(p_bottom, 1)
    r_top = shift(p_top, -1)
    p_top, p_bottom = products(plan, me, grads, [(1, 0, half, o_top), (3, half, rows, o_bottom)], weights)
    l_top = shift(p_top, 1)
    r_bottom = shift(p_bottom, -1)
    mine = products(plan, me, grads, [(0, 0, rows, None)], weights)[0]
    total = (
        mine.astype(F32)
        + jnp.concatenate([l_top, l_bottom], axis=0).astype(F32)
        + jnp.concatenate([r_top, r_bottom], axis=0).astype(F32)
    ).astype(BF16)
    total, back_direct = lax.optimization_barrier((total, back_direct))
    back_far = exchange(total)

    spread = choose * jnp.concatenate([weight, weight], axis=0)
    coarse = lax.reduce_precision(spread, 8, 7)
    fine = (spread - coarse).astype(BF16)
    coarse = coarse.astype(BF16)

    def mix(back):
        return dot(coarse, back) + dot(fine, back)

    mixed = mix(back_direct)
    near = mixed[:, :DIRECT]
    for k in range(1, parts):
        near = near + shift(mixed[:, k * DIRECT : (k + 1) * DIRECT].astype(BF16), k).astype(F32)
    result = jnp.concatenate([near.astype(BF16), mix(back_far).astype(BF16)], axis=1)
    return result[:toks], result[toks:]


def solution(mesh):
    return jax.shard_map(
        per_device,
        mesh=mesh,
        in_specs=(
            P("expert", "hidden"),
            P("expert", None),
            P("expert", None),
            P("expert", None, "hidden"),
            P("expert", None, "hidden"),
            P("expert", "hidden", None),
            P("expert", "hidden"),
        ),
        out_specs=(P("expert", "hidden"), P("expert", "hidden")),
        check_vma=False,
    )
```

```python
import jax
import jax.numpy as jnp
from jax import lax
from jax.experimental import pallas as pl
from jax.experimental.pallas import tpu as pltpu
from jax.sharding import PartitionSpec as P


DIRECT = 384
CAP = 4
LANES = 128
MIB = 1 << 20
F32, BF16 = jnp.float32, jnp.bfloat16
ANY = pl.BlockSpec(memory_space=pl.ANY)
HBM = pl.BlockSpec(memory_space=pltpu.HBM)
SMEM = pl.BlockSpec(memory_space=pltpu.SMEM)
VMEM = pl.BlockSpec(memory_space=pltpu.VMEM)


def dot(a, b):
    return jnp.dot(a, b, preferred_element_type=F32)


def dot_t(a, b):
    return lax.dot_general(a, b, (((1,), (1,)), ((), ())), preferred_element_type=F32)


class Plan:
    def __init__(self, parts, depth, width):
        self.parts, self.depth, self.width = parts, depth, width
        self.slice = depth // parts
        self.far = self.slice - DIRECT

    def weight_scratch(self, reach):
        w = self.width
        return [pltpu.VMEM((reach, w), BF16), pltpu.VMEM((reach, w), BF16), pltpu.VMEM((w, reach), BF16)]

    def copies(self, me_ref, k, lo, reach, hbm, bufs, sems, at=0):
        start = pl.multiple_of(((me_ref[0] + k) % self.parts) * self.slice + lo, LANES)
        here, there = pl.ds(at, reach), pl.ds(start, reach)
        return [
            pltpu.make_async_copy(hbm[0].at[there, :], bufs[0].at[here, :], sems.at[0]),
            pltpu.make_async_copy(hbm[1].at[there, :], bufs[1].at[here, :], sems.at[1]),
            pltpu.make_async_copy(hbm[2].at[:, there], bufs[2].at[:, here], sems.at[2]),
        ]


def run(copies):
    for c in copies:
        c.start()
    return copies


def done(copies):
    for c in copies:
        c.wait()


def forward(x, bufs):
    return dot(x, bufs[0][...]), dot(x, bufs[1][...]), dot_t(x, bufs[2][...])


def backward(h, bufs, width):
    return (
        dot_t(h[:, :width], bufs[0][...])
        + dot_t(h[:, width : 2 * width], bufs[1][...])
        + dot(h[:, 2 * width :], bufs[2][...])
    )


def call(kernel, outs, args, scratch, specs, flops, limit, out_specs=None):
    moved = sum(a.size * a.dtype.itemsize for a, s in zip(args, specs) if s is VMEM)
    return pl.pallas_call(
        kernel,
        in_specs=specs,
        out_specs=out_specs or [VMEM] * len(outs),
        out_shape=[
            pltpu.HBM(s, t) if spec is HBM else jax.ShapeDtypeStruct(s, t)
            for (s, t), spec in zip(outs, out_specs or [VMEM] * len(outs))
        ],
        scratch_shapes=scratch,
        compiler_params=pltpu.CompilerParams(vmem_limit_bytes=limit * MIB),
        cost_estimate=pl.CostEstimate(flops=flops, bytes_accessed=moved + 4 * MIB, transcendentals=0),
    )(*args)


def pack_far(tokens, routes, cotangent, rows):
    toks, picks = routes.shape
    group = 2 * CAP
    experts = rows // group
    far = tokens.shape[1] - DIRECT

    def kernel(tok_hbm, routes_hbm, cot_hbm, out_ref, select_ref, table_ref, routes_ref, sems):
        loads = run(
            [
                pltpu.make_async_copy(routes_hbm, routes_ref, sems.at[0]),
                pltpu.make_async_copy(tok_hbm, table_ref.at[:toks], sems.at[1]),
                pltpu.make_async_copy(cot_hbm, table_ref.at[toks:], sems.at[2]),
            ]
        )
        row = lax.broadcasted_iota(jnp.int32, (toks, rows), 1)
        expert = lax.broadcasted_iota(jnp.int32, (experts, toks), 0)
        loads[0].wait()
        wanted = routes_ref[0:1, :] == expert
        for k in range(1, picks):
            wanted = wanted | (routes_ref[k : k + 1, :] == expert)
        spread = lax.broadcasted_iota(jnp.int32, (experts, rows), 1) // group == lax.broadcasted_iota(
            jnp.int32, (experts, rows), 0
        )
        named = (
            lax.dot_general(
                wanted.astype(F32).astype(BF16),
                spread.astype(F32).astype(BF16),
                (((0,), (0,)), ((), ())),
                preferred_element_type=F32,
            )
            > 0.5
        )
        earlier = (
            lax.broadcasted_iota(jnp.int32, (toks, toks), 0)
            > lax.broadcasted_iota(jnp.int32, (toks, toks), 1)
        ).astype(BF16)
        rank = dot(earlier, named.astype(F32).astype(BF16)).astype(jnp.int32)
        placed = named & (rank == row % CAP)
        is_token = row % group < CAP
        one, none = jnp.ones((toks, rows), F32), jnp.zeros((toks, rows), F32)
        select = jnp.concatenate(
            [jnp.where(placed & is_token, one, none), jnp.where(placed & ~is_token, one, none)], axis=0
        ).astype(BF16)
        select_ref[...] = select
        done(loads[1:])
        table = table_ref[:, DIRECT:]
        out_ref[...] = lax.dot_general(
            select, table, (((0,), (0,)), ((), ())), preferred_element_type=F32
        ).astype(BF16)

    return call(
        kernel,
        [((rows, far), BF16), ((2 * toks, rows), BF16)],
        [pltpu.with_memory_space_constraint(v, pltpu.HBM) for v in (tokens, routes.T, cotangent)],
        [
            pltpu.VMEM((2 * toks, tokens.shape[1]), BF16),
            pltpu.VMEM((picks, toks), jnp.int32),
            pltpu.SemaphoreType.DMA((3,)),
        ],
        [HBM] * 3,
        4 * toks * rows * far,
        12,
    )


def partial_sums(plan, me, sources, sums, weights, limit):
    w = plan.width
    xs = [x for _, pieces in sources for x in pieces]
    rows = sum(x.shape[0] for x in sources[0][1])
    base = [] if sums is None else [sums]

    def kernel(me_ref, *refs):
        base_refs, x_refs = refs[: len(base)], list(refs[len(base) : len(base) + len(xs)])
        wg, wu, wd, out_ref = refs[len(base) + len(xs) : len(base) + len(xs) + 4]
        bufs, sems = refs[len(base) + len(xs) + 4 : -1], refs[-1]
        loads = [
            run(plan.copies(me_ref, k, DIRECT, plan.far, (wg, wu, wd), bufs[3 * i : 3 * i + 3], sems.at[i]))
            for i, (k, _) in enumerate(sources)
        ]
        for i, (_, pieces) in enumerate(sources):
            done(loads[i])
            first = 0
            for _ in pieces:
                x = x_refs.pop(0)
                last = first + x.shape[0]
                for t, term in enumerate(forward(x[...], bufs[3 * i : 3 * i + 3])):
                    cols = slice(t * w, (t + 1) * w)
                    if i > 0:
                        term = term + out_ref[first:last, cols]
                    elif base_refs:
                        term = term + base_refs[0][first:last, cols]
                    out_ref[first:last, cols] = term
                first = last

    return call(
        kernel,
        [((rows, 3 * w), F32)],
        (me, *base, *xs, *weights),
        plan.weight_scratch(plan.far) * len(sources) + [pltpu.SemaphoreType.DMA((len(sources), 3))],
        [SMEM] + [VMEM] * (len(base) + len(xs)) + [HBM] * 3,
        2 * rows * 3 * w * plan.far * len(sources),
        limit,
    )[0]


def gates(plan, me, sums, arrived, weights):
    rows, w = sums.shape[0], plan.width
    half, block = rows // 2, 128
    order = (2,)
    n = len(order)
    near_cols = plan.parts * DIRECT

    def kernel(me_ref, sums_hbm, *refs):
        x_hbm, (wg, wu, wd, out_ref, top_ref, bottom_ref, near_ref), rest = (
            refs[: 2 * n],
            refs[2 * n : 2 * n + 7],
            refs[2 * n + 7 :],
        )
        acc, x_buf, direct_buf = rest[:3]
        near, far, (n_sems, f_sems, x_sems, m_sems) = rest[3:6], rest[6:-4], rest[-4:]
        hbm = (wg, wu, wd)
        first_load = pltpu.make_async_copy(sums_hbm, acc, m_sems.at[0])
        first_load.start()
        loads = []
        for i, k in enumerate(order):
            weight_loads = run(plan.copies(me_ref, k, DIRECT, plan.far, hbm, far[3 * i : 3 * i + 3], f_sems.at[i]))
            x_loads = run(
                [pltpu.make_async_copy(x_hbm[2 * i + j], x_buf.at[2 * i + j], x_sems.at[2 * i + j]) for j in range(2)]
            )
            loads.append(weight_loads + x_loads)
        near_loads = [
            c
            for k in range(plan.parts)
            for c in run(plan.copies(me_ref, k, 0, DIRECT, hbm, near, n_sems.at[k], k * DIRECT))
        ]
        first_load.wait()
        for i in range(n):
            done(loads[i])
            for j in range(2):
                for t, term in enumerate(forward(x_buf[2 * i + j], far[3 * i : 3 * i + 3])):
                    acc[j * half : (j + 1) * half, t * w : (t + 1) * w] += term

        @pl.loop(0, rows // block)
        def _(b):
            r = pl.ds(pl.multiple_of(b * block, block), block)
            gate, up = acc[r, 0:w], acc[r, w : 2 * w]
            back = pltpu.roll(acc[r, 2 * w : 3 * w], block - CAP, 0)
            first = lax.broadcasted_iota(jnp.int32, (block, w), 0) % (2 * CAP) < CAP
            sig = jax.nn.sigmoid(gate)
            act = gate * sig
            zero = jnp.zeros_like(act)
            grad_gate = back * up * sig * (1.0 + gate * (1.0 - sig))
            grad_up = back * act
            out_ref[r, 0:w] = jnp.where(first, zero, pltpu.roll(grad_gate, CAP, 0)).astype(BF16)
            out_ref[r, w : 2 * w] = jnp.where(first, zero, pltpu.roll(grad_up, CAP, 0)).astype(BF16)
            out_ref[r, 2 * w : 3 * w] = jnp.where(first, act * up, zero).astype(BF16)

        done(near_loads)
        direct_buf[...] = backward(out_ref[...], near, w).astype(BF16)
        store = pltpu.make_async_copy(direct_buf, near_ref, m_sems.at[2])
        store.start()
        relay = backward(out_ref[...], far[-3:], w).astype(BF16)
        top_ref[...] = relay[:half]
        bottom_ref[...] = relay[half:]
        store.wait()

    scratch = [
        pltpu.VMEM((rows, 3 * w), F32),
        pltpu.VMEM((2 * n, half, plan.far), BF16),
        pltpu.VMEM((rows, near_cols), BF16),
        *plan.weight_scratch(near_cols),
        *(plan.weight_scratch(plan.far) * n),
        pltpu.SemaphoreType.DMA((plan.parts, 3)),
        pltpu.SemaphoreType.DMA((n, 3)),
        pltpu.SemaphoreType.DMA((2 * n,)),
        pltpu.SemaphoreType.DMA((3,)),
    ]
    out = call(
        kernel,
        [
            ((rows, 3 * w), BF16),
            ((half, plan.far), BF16),
            ((half, plan.far), BF16),
            ((rows, near_cols), BF16),
        ],
        (me, sums, *arrived, *weights),
        scratch,
        [SMEM] + [ANY] * (2 * n + 1) + [HBM] * 3,
        2 * rows * 3 * w * ((n + 1) * plan.far + near_cols),
        26,
        [VMEM, VMEM, VMEM, HBM],
    )
    return out


def near_sums(plan, me, sums, direct, weights):
    rows, w = sums.shape[0], plan.width
    near_cols = plan.parts * DIRECT

    def kernel(me_ref, sums_ref, x_ref, wg, wu, wd, out_ref, g, u, d, sems):
        loads = []
        for k in range(plan.parts):
            loads += run(plan.copies(me_ref, k, 0, DIRECT, (wg, wu, wd), (g, u, d), sems.at[k], k * DIRECT))
        done(loads)
        for t, term in enumerate(forward(x_ref[...], (g, u, d))):
            c = slice(t * w, (t + 1) * w)
            out_ref[:, c] = sums_ref[:, c] + term

    return call(
        kernel,
        [((rows, 3 * w), F32)],
        (me, sums, direct, *weights),
        plan.weight_scratch(near_cols) + [pltpu.SemaphoreType.DMA((plan.parts, 3))],
        [SMEM, VMEM, VMEM, HBM, HBM, HBM],
        2 * rows * 3 * w * near_cols,
        16,
    )[0]


def products(plan, me, h, wanted, weights):
    w = plan.width
    reach = plan.far
    adds = [a for *_, a in wanted if a is not None]
    outs = [((last - first, reach), BF16) for _, first, last, _ in wanted]

    def kernel(me_ref, h_ref, *refs):
        add_refs = list(refs[: len(adds)])
        wg, wu, wd = refs[len(adds) : len(adds) + 3]
        out_refs = refs[len(adds) + 3 : len(adds) + 3 + len(outs)]
        bufs, sems = refs[len(adds) + 3 + len(outs) : -1], refs[-1]
        loads = [
            run(plan.copies(me_ref, k, DIRECT, reach, (wg, wu, wd), bufs[3 * i : 3 * i + 3], sems.at[i]))
            for i, (k, *_) in enumerate(wanted)
        ]
        for i, (_, first, last, extra) in enumerate(wanted):
            done(loads[i])
            value = backward(h_ref[first:last, :], bufs[3 * i : 3 * i + 3], w)
            if extra is not None:
                value = value + add_refs.pop(0)[...].astype(F32)
            out_refs[i][...] = value.astype(BF16)

    return call(
        kernel,
        outs,
        (me, h, *adds, *weights),
        plan.weight_scratch(reach) * len(wanted) + [pltpu.SemaphoreType.DMA((len(wanted), 3))],
        [SMEM] + [VMEM] * (1 + len(adds)) + [HBM] * 3,
        sum(2 * (last - first) * 3 * w * reach for _, first, last, _ in wanted),
        16,
    )


def per_device(tokens, routes, combine, w_gate, w_up, w_down, cotangent):
    toks, _ = tokens.shape
    sources = lax.axis_size("expert")
    parts = lax.axis_size("hidden")
    group = 2 * CAP
    rows = sources * group
    half = rows // 2
    plan = Plan(parts, w_gate.shape[1], w_gate.shape[2])
    me = lax.axis_index("hidden").astype(jnp.int32).reshape(1)
    weights = tuple(
        pltpu.with_memory_space_constraint(w[0], pltpu.HBM) for w in (w_gate, w_up, w_down)
    )

    def shift(v, k):
        return lax.ppermute(v, "hidden", [(i, (i + k) % parts) for i in range(parts)])

    def exchange(v):
        out = lax.all_to_all(
            v.reshape(sources, group, v.shape[1]), "expert", split_axis=0, concat_axis=0, tiled=True
        )
        return out.reshape(rows, v.shape[1])

    direct = jnp.concatenate([tokens[:, :DIRECT], cotangent[:, :DIRECT]], axis=0)
    direct_parts = [direct] + [shift(direct, parts - k) for k in range(1, parts)]

    packed_far, select = pack_far(tokens, routes, cotangent, rows)

    def pack(values):
        return lax.dot_general(
            select, values, (((0,), (0,)), ((), ())), preferred_element_type=F32
        ).astype(BF16)

    own = exchange(packed_far)
    packed_direct = pack(jnp.concatenate(direct_parts, axis=1))
    own, packed_direct = lax.optimization_barrier((own, packed_direct))
    top, bottom = own[:half], own[half:]
    l_top = shift(top, 1)
    r_bottom = shift(bottom, -1)
    arrived_direct = exchange(packed_direct)
    l_bottom = shift(bottom, 1)
    r_top = shift(top, -1)
    o_top = shift(l_top, 1)
    o_bottom = shift(r_bottom, -1)
    sums = partial_sums(plan, me, [(0, [own])], None, weights, 14)
    sums = partial_sums(plan, me, [(3, [l_top, l_bottom]), (1, [r_top, r_bottom])], sums, weights, 18)
    sums = near_sums(plan, me, sums, arrived_direct, weights)
    grads, relay_top, relay_bottom, near = gates(plan, me, sums, (o_top, o_bottom), weights)

    o_top = shift(relay_top, 1)
    o_bottom = shift(relay_bottom, -1)
    back_direct = exchange(near)
    p_bottom, p_top = products(plan, me, grads, [(1, half, rows, None), (3, 0, half, None)], weights)
    l_bottom = shift(p_bottom, 1)
    r_top = shift(p_top, -1)
    p_top, p_bottom = products(plan, me, grads, [(1, 0, half, o_top), (3, half, rows, o_bottom)], weights)
    l_top = shift(p_top, 1)
    r_bottom = shift(p_bottom, -1)
    mine = products(plan, me, grads, [(0, 0, rows, None)], weights)[0]
    total = (
        mine.astype(F32)
        + jnp.concatenate([l_top, l_bottom], axis=0).astype(F32)
        + jnp.concatenate([r_top, r_bottom], axis=0).astype(F32)
    ).astype(BF16)
    total, back_direct = lax.optimization_barrier((total, back_direct))
    back_far = exchange(total)

    owner = lax.broadcasted_iota(jnp.int32, (toks, rows), 1) // group
    hit = routes[:, :, None] == owner[:, None, :]
    weight = jnp.sum(jnp.where(hit, combine[:, :, None], 0.0), axis=1)
    spread = select.astype(F32) * jnp.concatenate([weight, weight], axis=0)
    coarse = lax.reduce_precision(spread, 8, 7)
    fine = (spread - coarse).astype(BF16)
    coarse = coarse.astype(BF16)

    def mix(back):
        return dot(coarse, back) + dot(fine, back)

    mixed = mix(back_direct)
    near = mixed[:, :DIRECT]
    for k in range(1, parts):
        near = near + shift(mixed[:, k * DIRECT : (k + 1) * DIRECT].astype(BF16), k).astype(F32)
    result = jnp.concatenate([near.astype(BF16), mix(back_far).astype(BF16)], axis=1)
    return result[:toks], result[toks:]


def solution(mesh):
    return jax.shard_map(
        per_device,
        mesh=mesh,
        in_specs=(
            P("expert", "hidden"),
            P("expert", None),
            P("expert", None),
            P("expert", None, "hidden"),
            P("expert", None, "hidden"),
            P("expert", "hidden", None),
            P("expert", "hidden"),
        ),
        out_specs=(P("expert", "hidden"), P("expert", "hidden")),
        check_vma=False,
    )
```

```python
import jax
import jax.numpy as jnp
from jax import lax
from jax.experimental import pallas as pl
from jax.experimental.pallas import tpu as pltpu
from jax.sharding import PartitionSpec as P


DIRECT = 384
CAP = 4
LANES = 128
MIB = 1 << 20
F32, BF16 = jnp.float32, jnp.bfloat16
ANY = pl.BlockSpec(memory_space=pl.ANY)
HBM = pl.BlockSpec(memory_space=pltpu.HBM)
SMEM = pl.BlockSpec(memory_space=pltpu.SMEM)
VMEM = pl.BlockSpec(memory_space=pltpu.VMEM)
KEPT = pl.BlockSpec(memory_space=pltpu.VMEM)


def dot(a, b):
    return jnp.dot(a, b, preferred_element_type=F32)


def dot_t(a, b):
    return lax.dot_general(a, b, (((1,), (1,)), ((), ())), preferred_element_type=F32)


class Plan:
    def __init__(self, parts, depth, width):
        self.parts, self.depth, self.width = parts, depth, width
        self.slice = depth // parts
        self.far = self.slice - DIRECT

    def weight_scratch(self, reach):
        w = self.width
        return [pltpu.VMEM((reach, w), BF16), pltpu.VMEM((reach, w), BF16), pltpu.VMEM((w, reach), BF16)]

    def copies(self, me_ref, k, lo, reach, hbm, bufs, sems, at=0):
        start = pl.multiple_of(((me_ref[0] + k) % self.parts) * self.slice + lo, LANES)
        here, there = pl.ds(at, reach), pl.ds(start, reach)
        return [
            pltpu.make_async_copy(hbm[0].at[there, :], bufs[0].at[here, :], sems.at[0]),
            pltpu.make_async_copy(hbm[1].at[there, :], bufs[1].at[here, :], sems.at[1]),
            pltpu.make_async_copy(hbm[2].at[:, there], bufs[2].at[:, here], sems.at[2]),
        ]


def run(copies):
    for c in copies:
        c.start()
    return copies


def done(copies):
    for c in copies:
        c.wait()


def forward(x, bufs):
    return dot(x, bufs[0][...]), dot(x, bufs[1][...]), dot_t(x, bufs[2][...])


def backward(h, bufs, width):
    return (
        dot_t(h[:, :width], bufs[0][...])
        + dot_t(h[:, width : 2 * width], bufs[1][...])
        + dot(h[:, 2 * width :], bufs[2][...])
    )


def call(kernel, outs, args, scratch, specs, flops, limit, out_specs=None):
    moved = sum(a.size * a.dtype.itemsize for a, s in zip(args, specs) if s is VMEM)
    return pl.pallas_call(
        kernel,
        in_specs=specs,
        out_specs=out_specs or [VMEM] * len(outs),
        out_shape=[
            pltpu.HBM(s, t) if spec is HBM else pltpu.VMEM(s, t) if spec is KEPT else jax.ShapeDtypeStruct(s, t)
            for (s, t), spec in zip(outs, out_specs or [VMEM] * len(outs))
        ],
        scratch_shapes=scratch,
        compiler_params=pltpu.CompilerParams(vmem_limit_bytes=limit * MIB),
        cost_estimate=pl.CostEstimate(flops=flops, bytes_accessed=moved + 4 * MIB, transcendentals=0),
    )(*args)


def pack_far(tokens, routes, cotangent, rows):
    toks, picks = routes.shape
    group = 2 * CAP
    experts = rows // group
    far = tokens.shape[1] - DIRECT

    def kernel(tok_hbm, routes_hbm, cot_hbm, out_ref, select_ref, table_ref, routes_ref, sems):
        loads = run(
            [
                pltpu.make_async_copy(routes_hbm, routes_ref, sems.at[0]),
                pltpu.make_async_copy(tok_hbm, table_ref.at[:toks], sems.at[1]),
                pltpu.make_async_copy(cot_hbm, table_ref.at[toks:], sems.at[2]),
            ]
        )
        row = lax.broadcasted_iota(jnp.int32, (toks, rows), 1)
        expert = lax.broadcasted_iota(jnp.int32, (experts, toks), 0)
        loads[0].wait()
        wanted = routes_ref[0:1, :] == expert
        for k in range(1, picks):
            wanted = wanted | (routes_ref[k : k + 1, :] == expert)
        spread = lax.broadcasted_iota(jnp.int32, (experts, rows), 1) // group == lax.broadcasted_iota(
            jnp.int32, (experts, rows), 0
        )
        named = (
            lax.dot_general(
                wanted.astype(F32).astype(BF16),
                spread.astype(F32).astype(BF16),
                (((0,), (0,)), ((), ())),
                preferred_element_type=F32,
            )
            > 0.5
        )
        earlier = (
            lax.broadcasted_iota(jnp.int32, (toks, toks), 0)
            > lax.broadcasted_iota(jnp.int32, (toks, toks), 1)
        ).astype(BF16)
        rank = dot(earlier, named.astype(F32).astype(BF16)).astype(jnp.int32)
        placed = named & (rank == row % CAP)
        is_token = row % group < CAP
        one, none = jnp.ones((toks, rows), F32), jnp.zeros((toks, rows), F32)
        select = jnp.concatenate(
            [jnp.where(placed & is_token, one, none), jnp.where(placed & ~is_token, one, none)], axis=0
        ).astype(BF16)
        select_ref[...] = select
        done(loads[1:])
        table = table_ref[:, DIRECT:]
        out_ref[...] = lax.dot_general(
            select, table, (((0,), (0,)), ((), ())), preferred_element_type=F32
        ).astype(BF16)

    return call(
        kernel,
        [((rows, far), BF16), ((2 * toks, rows), BF16)],
        [pltpu.with_memory_space_constraint(v, pltpu.HBM) for v in (tokens, routes.T, cotangent)],
        [
            pltpu.VMEM((2 * toks, tokens.shape[1]), BF16),
            pltpu.VMEM((picks, toks), jnp.int32),
            pltpu.SemaphoreType.DMA((3,)),
        ],
        [HBM] * 3,
        4 * toks * rows * far,
        12,
    )


def partial_sums(plan, me, sources, sums, weights, limit):
    w = plan.width
    xs = [x for _, pieces in sources for x in pieces]
    rows = sum(x.shape[0] for x in sources[0][1])
    base = [] if sums is None else [sums]

    def kernel(me_ref, *refs):
        base_refs, x_refs = refs[: len(base)], list(refs[len(base) : len(base) + len(xs)])
        wg, wu, wd, out_ref = refs[len(base) + len(xs) : len(base) + len(xs) + 4]
        bufs, sems = refs[len(base) + len(xs) + 4 : -1], refs[-1]
        loads = [
            run(plan.copies(me_ref, k, DIRECT, plan.far, (wg, wu, wd), bufs[3 * i : 3 * i + 3], sems.at[i]))
            for i, (k, _) in enumerate(sources)
        ]
        for i, (_, pieces) in enumerate(sources):
            done(loads[i])
            first = 0
            for _ in pieces:
                x = x_refs.pop(0)
                last = first + x.shape[0]
                for t, term in enumerate(forward(x[...], bufs[3 * i : 3 * i + 3])):
                    cols = slice(t * w, (t + 1) * w)
                    if i > 0:
                        term = term + out_ref[first:last, cols]
                    elif base_refs:
                        term = term + base_refs[0][first:last, cols]
                    out_ref[first:last, cols] = term
                first = last

    return call(
        kernel,
        [((rows, 3 * w), F32)],
        (me, *base, *xs, *weights),
        plan.weight_scratch(plan.far) * len(sources) + [pltpu.SemaphoreType.DMA((len(sources), 3))],
        [SMEM] + [VMEM] * (len(base) + len(xs)) + [HBM] * 3,
        2 * rows * 3 * w * plan.far * len(sources),
        limit,
    )[0]


def gates(plan, me, sums, arrived, weights):
    rows, w = sums.shape[0], plan.width
    half, block = rows // 2, 128
    order = (2,)
    n = len(order)
    near_cols = plan.parts * DIRECT

    def kernel(me_ref, sums_hbm, *refs):
        x_hbm, (wg, wu, wd, out_ref, top_ref, bottom_ref, near_ref), rest = (
            refs[: 2 * n],
            refs[2 * n : 2 * n + 7],
            refs[2 * n + 7 :],
        )
        acc, x_buf, direct_buf = rest[:3]
        near, far, (n_sems, f_sems, x_sems, m_sems) = rest[3:6], rest[6:-4], rest[-4:]
        hbm = (wg, wu, wd)
        first_load = pltpu.make_async_copy(sums_hbm, acc, m_sems.at[0])
        first_load.start()
        loads = []
        for i, k in enumerate(order):
            weight_loads = run(plan.copies(me_ref, k, DIRECT, plan.far, hbm, far[3 * i : 3 * i + 3], f_sems.at[i]))
            x_loads = run(
                [pltpu.make_async_copy(x_hbm[2 * i + j], x_buf.at[2 * i + j], x_sems.at[2 * i + j]) for j in range(2)]
            )
            loads.append(weight_loads + x_loads)
        first_load.wait()
        for i in range(n):
            done(loads[i])
            near_loads = [
                c
                for k in range(plan.parts)
                for c in run(plan.copies(me_ref, k, 0, DIRECT, hbm, near, n_sems.at[k], k * DIRECT))
            ]
            for j in range(2):
                for t, term in enumerate(forward(x_buf[2 * i + j], far[3 * i : 3 * i + 3])):
                    acc[j * half : (j + 1) * half, t * w : (t + 1) * w] += term

        @pl.loop(0, rows // block)
        def _(b):
            r = pl.ds(pl.multiple_of(b * block, block), block)
            gate, up = acc[r, 0:w], acc[r, w : 2 * w]
            back = pltpu.roll(acc[r, 2 * w : 3 * w], block - CAP, 0)
            first = lax.broadcasted_iota(jnp.int32, (block, w), 0) % (2 * CAP) < CAP
            sig = jax.nn.sigmoid(gate)
            act = gate * sig
            zero = jnp.zeros_like(act)
            grad_gate = back * up * sig * (1.0 + gate * (1.0 - sig))
            grad_up = back * act
            out_ref[r, 0:w] = jnp.where(first, zero, pltpu.roll(grad_gate, CAP, 0)).astype(BF16)
            out_ref[r, w : 2 * w] = jnp.where(first, zero, pltpu.roll(grad_up, CAP, 0)).astype(BF16)
            out_ref[r, 2 * w : 3 * w] = jnp.where(first, act * up, zero).astype(BF16)

        done(near_loads)
        direct_buf[...] = backward(out_ref[...], near, w).astype(BF16)
        store = pltpu.make_async_copy(direct_buf, near_ref, m_sems.at[2])
        store.start()
        relay = backward(out_ref[...], far[-3:], w).astype(BF16)
        top_ref[...] = relay[:half]
        bottom_ref[...] = relay[half:]
        store.wait()

    scratch = [
        pltpu.VMEM((rows, 3 * w), F32),
        pltpu.VMEM((2 * n, half, plan.far), BF16),
        pltpu.VMEM((rows, near_cols), BF16),
        *plan.weight_scratch(near_cols),
        *(plan.weight_scratch(plan.far) * n),
        pltpu.SemaphoreType.DMA((plan.parts, 3)),
        pltpu.SemaphoreType.DMA((n, 3)),
        pltpu.SemaphoreType.DMA((2 * n,)),
        pltpu.SemaphoreType.DMA((3,)),
    ]
    out = call(
        kernel,
        [
            ((rows, 3 * w), BF16),
            ((half, plan.far), BF16),
            ((half, plan.far), BF16),
            ((rows, near_cols), BF16),
        ],
        (me, sums, *arrived, *weights),
        scratch,
        [SMEM] + [ANY] * (2 * n + 1) + [HBM] * 3,
        2 * rows * 3 * w * ((n + 1) * plan.far + near_cols),
        26,
        [VMEM, KEPT, KEPT, HBM],
    )
    return out


def near_sums(plan, me, sums, direct, weights):
    rows, w = sums.shape[0], plan.width
    near_cols = plan.parts * DIRECT

    def kernel(me_ref, sums_ref, x_hbm, wg, wu, wd, out_ref, x_ref, g, u, d, sems, x_sem):
        loads = run([pltpu.make_async_copy(x_hbm, x_ref, x_sem.at[0])])
        for k in range(plan.parts):
            loads += run(plan.copies(me_ref, k, 0, DIRECT, (wg, wu, wd), (g, u, d), sems.at[k], k * DIRECT))
        done(loads)
        for t, term in enumerate(forward(x_ref[...], (g, u, d))):
            c = slice(t * w, (t + 1) * w)
            out_ref[:, c] = sums_ref[:, c] + term

    return call(
        kernel,
        [((rows, 3 * w), F32)],
        (me, sums, direct, *weights),
        [pltpu.VMEM((rows, near_cols), BF16)]
        + plan.weight_scratch(near_cols)
        + [pltpu.SemaphoreType.DMA((plan.parts, 3)), pltpu.SemaphoreType.DMA((1,))],
        [SMEM, VMEM, ANY, HBM, HBM, HBM],
        2 * rows * 3 * w * near_cols,
        16,
    )[0]


def products(plan, me, h, wanted, weights):
    w = plan.width
    reach = plan.far
    adds = [a for *_, a in wanted if a is not None]
    outs = [((last - first, reach), BF16) for _, first, last, _ in wanted]

    def kernel(me_ref, h_ref, *refs):
        add_refs = list(refs[: len(adds)])
        wg, wu, wd = refs[len(adds) : len(adds) + 3]
        out_refs = refs[len(adds) + 3 : len(adds) + 3 + len(outs)]
        bufs, sems = refs[len(adds) + 3 + len(outs) : -1], refs[-1]
        loads = [
            run(plan.copies(me_ref, k, DIRECT, reach, (wg, wu, wd), bufs[3 * i : 3 * i + 3], sems.at[i]))
            for i, (k, *_) in enumerate(wanted)
        ]
        for i, (_, first, last, extra) in enumerate(wanted):
            done(loads[i])
            value = backward(h_ref[first:last, :], bufs[3 * i : 3 * i + 3], w)
            if extra is not None:
                value = value + add_refs.pop(0)[...].astype(F32)
            out_refs[i][...] = value.astype(BF16)

    return call(
        kernel,
        outs,
        (me, h, *adds, *weights),
        plan.weight_scratch(reach) * len(wanted) + [pltpu.SemaphoreType.DMA((len(wanted), 3))],
        [SMEM] + [VMEM] * (1 + len(adds)) + [HBM] * 3,
        sum(2 * (last - first) * 3 * w * reach for _, first, last, _ in wanted),
        16,
    )


def per_device(tokens, routes, combine, w_gate, w_up, w_down, cotangent):
    toks, _ = tokens.shape
    sources = lax.axis_size("expert")
    parts = lax.axis_size("hidden")
    group = 2 * CAP
    rows = sources * group
    half = rows // 2
    plan = Plan(parts, w_gate.shape[1], w_gate.shape[2])
    me = lax.axis_index("hidden").astype(jnp.int32).reshape(1)
    weights = tuple(
        pltpu.with_memory_space_constraint(w[0], pltpu.HBM) for w in (w_gate, w_up, w_down)
    )

    def shift(v, k):
        return lax.ppermute(v, "hidden", [(i, (i + k) % parts) for i in range(parts)])

    def exchange(v):
        out = lax.all_to_all(
            v.reshape(sources, group, v.shape[1]), "expert", split_axis=0, concat_axis=0, tiled=True
        )
        return out.reshape(rows, v.shape[1])

    direct = jnp.concatenate([tokens[:, :DIRECT], cotangent[:, :DIRECT]], axis=0)
    direct_parts = [direct] + [shift(direct, parts - k) for k in range(1, parts)]

    packed_far, select = pack_far(tokens, routes, cotangent, rows)

    def pack(values):
        return lax.dot_general(
            select, values, (((0,), (0,)), ((), ())), preferred_element_type=F32
        ).astype(BF16)

    own = exchange(packed_far)
    packed_direct = pack(jnp.concatenate(direct_parts, axis=1))
    own, packed_direct = lax.optimization_barrier((own, packed_direct))
    top, bottom = own[:half], own[half:]
    l_top = shift(top, 1)
    r_bottom = shift(bottom, -1)
    arrived_direct = exchange(packed_direct)
    l_bottom = shift(bottom, 1)
    r_top = shift(top, -1)
    o_top = shift(l_top, 1)
    o_bottom = shift(r_bottom, -1)
    sums = partial_sums(plan, me, [(0, [own])], None, weights, 14)
    sums = partial_sums(plan, me, [(3, [l_top, l_bottom]), (1, [r_top, r_bottom])], sums, weights, 18)
    sums = near_sums(plan, me, sums, arrived_direct, weights)
    grads, relay_top, relay_bottom, near = gates(plan, me, sums, (o_top, o_bottom), weights)

    o_top = shift(relay_top, 1)
    o_bottom = shift(relay_bottom, -1)
    back_direct = exchange(near)
    p_bottom, p_top = products(plan, me, grads, [(1, half, rows, None), (3, 0, half, None)], weights)
    l_bottom = shift(p_bottom, 1)
    r_top = shift(p_top, -1)
    p_top, p_bottom = products(plan, me, grads, [(1, 0, half, o_top), (3, half, rows, o_bottom)], weights)
    l_top = shift(p_top, 1)
    r_bottom = shift(p_bottom, -1)
    mine = products(plan, me, grads, [(0, 0, rows, None)], weights)[0]
    total = (
        mine.astype(F32)
        + jnp.concatenate([l_top, l_bottom], axis=0).astype(F32)
        + jnp.concatenate([r_top, r_bottom], axis=0).astype(F32)
    ).astype(BF16)
    total, back_direct = lax.optimization_barrier((total, back_direct))
    back_far = exchange(total)

    owner = lax.broadcasted_iota(jnp.int32, (toks, rows), 1) // group
    hit = routes[:, :, None] == owner[:, None, :]
    weight = jnp.sum(jnp.where(hit, combine[:, :, None], 0.0), axis=1)
    spread = select.astype(F32) * jnp.concatenate([weight, weight], axis=0)
    coarse = lax.reduce_precision(spread, 8, 7)
    fine = (spread - coarse).astype(BF16)
    coarse = coarse.astype(BF16)

    def mix(back):
        return dot(coarse, back) + dot(fine, back)

    mixed = mix(back_direct)
    near = mixed[:, :DIRECT]
    for k in range(1, parts):
        near = near + shift(mixed[:, k * DIRECT : (k + 1) * DIRECT].astype(BF16), k).astype(F32)
    result = jnp.concatenate([near.astype(BF16), mix(back_far).astype(BF16)], axis=1)
    return result[:toks], result[toks:]


def solution(mesh):
    return jax.shard_map(
        per_device,
        mesh=mesh,
        in_specs=(
            P("expert", "hidden"),
            P("expert", None),
            P("expert", None),
            P("expert", None, "hidden"),
            P("expert", None, "hidden"),
            P("expert", "hidden", None),
            P("expert", "hidden"),
        ),
        out_specs=(P("expert", "hidden"), P("expert", "hidden")),
        check_vma=False,
    )
```

```python
import jax
import jax.numpy as jnp
from jax import lax
from jax.experimental import pallas as pl
from jax.experimental.pallas import tpu as pltpu
from jax.sharding import PartitionSpec as P


DIRECT = 384
CAP = 4
LANES = 128
MIB = 1 << 20
F32, BF16 = jnp.float32, jnp.bfloat16
ANY = pl.BlockSpec(memory_space=pl.ANY)
HBM = pl.BlockSpec(memory_space=pltpu.HBM)
SMEM = pl.BlockSpec(memory_space=pltpu.SMEM)
VMEM = pl.BlockSpec(memory_space=pltpu.VMEM)
KEPT = pl.BlockSpec(memory_space=pltpu.VMEM)


def dot(a, b):
    return jnp.dot(a, b, preferred_element_type=F32)


def dot_t(a, b):
    return lax.dot_general(a, b, (((1,), (1,)), ((), ())), preferred_element_type=F32)


class Plan:
    def __init__(self, parts, depth, width):
        self.parts, self.depth, self.width = parts, depth, width
        self.slice = depth // parts
        self.far = self.slice - DIRECT

    def weight_scratch(self, reach):
        w = self.width
        return [pltpu.VMEM((reach, w), BF16), pltpu.VMEM((reach, w), BF16), pltpu.VMEM((w, reach), BF16)]

    def copies(self, me_ref, k, lo, reach, hbm, bufs, sems, at=0):
        start = pl.multiple_of(((me_ref[0] + k) % self.parts) * self.slice + lo, LANES)
        here, there = pl.ds(at, reach), pl.ds(start, reach)
        return [
            pltpu.make_async_copy(hbm[0].at[there, :], bufs[0].at[here, :], sems.at[0]),
            pltpu.make_async_copy(hbm[1].at[there, :], bufs[1].at[here, :], sems.at[1]),
            pltpu.make_async_copy(hbm[2].at[:, there], bufs[2].at[:, here], sems.at[2]),
        ]


def run(copies):
    for c in copies:
        c.start()
    return copies


def done(copies):
    for c in copies:
        c.wait()


def forward(x, bufs):
    return dot(x, bufs[0][...]), dot(x, bufs[1][...]), dot_t(x, bufs[2][...])


def forward_one(x, bufs, t):
    return dot_t(x, bufs[2][...]) if t == 2 else dot(x, bufs[t][...])


def backward(h, bufs, width):
    return (
        dot_t(h[:, :width], bufs[0][...])
        + dot_t(h[:, width : 2 * width], bufs[1][...])
        + dot(h[:, 2 * width :], bufs[2][...])
    )


def call(kernel, outs, args, scratch, specs, flops, limit, out_specs=None):
    moved = sum(a.size * a.dtype.itemsize for a, s in zip(args, specs) if s is VMEM)
    return pl.pallas_call(
        kernel,
        in_specs=specs,
        out_specs=out_specs or [VMEM] * len(outs),
        out_shape=[
            pltpu.HBM(s, t) if spec is HBM else pltpu.VMEM(s, t) if spec is KEPT else jax.ShapeDtypeStruct(s, t)
            for (s, t), spec in zip(outs, out_specs or [VMEM] * len(outs))
        ],
        scratch_shapes=scratch,
        compiler_params=pltpu.CompilerParams(vmem_limit_bytes=limit * MIB),
        cost_estimate=pl.CostEstimate(flops=flops, bytes_accessed=moved + 4 * MIB, transcendentals=0),
    )(*args)


def pack_far(tokens, routes, cotangent, rows):
    toks, picks = routes.shape
    group = 2 * CAP
    experts = rows // group
    far = tokens.shape[1] - DIRECT

    def kernel(tok_hbm, routes_hbm, cot_hbm, out_ref, select_ref, table_ref, routes_ref, sems):
        loads = run(
            [
                pltpu.make_async_copy(routes_hbm, routes_ref, sems.at[0]),
                pltpu.make_async_copy(tok_hbm, table_ref.at[:toks], sems.at[1]),
                pltpu.make_async_copy(cot_hbm, table_ref.at[toks:], sems.at[2]),
            ]
        )
        row = lax.broadcasted_iota(jnp.int32, (toks, rows), 1)
        expert = lax.broadcasted_iota(jnp.int32, (experts, toks), 0)
        loads[0].wait()
        wanted = routes_ref[0:1, :] == expert
        for k in range(1, picks):
            wanted = wanted | (routes_ref[k : k + 1, :] == expert)
        spread = lax.broadcasted_iota(jnp.int32, (experts, rows), 1) // group == lax.broadcasted_iota(
            jnp.int32, (experts, rows), 0
        )
        named = (
            lax.dot_general(
                wanted.astype(F32).astype(BF16),
                spread.astype(F32).astype(BF16),
                (((0,), (0,)), ((), ())),
                preferred_element_type=F32,
            )
            > 0.5
        )
        earlier = (
            lax.broadcasted_iota(jnp.int32, (toks, toks), 0)
            > lax.broadcasted_iota(jnp.int32, (toks, toks), 1)
        ).astype(BF16)
        rank = dot(earlier, named.astype(F32).astype(BF16)).astype(jnp.int32)
        placed = named & (rank == row % CAP)
        is_token = row % group < CAP
        one, none = jnp.ones((toks, rows), F32), jnp.zeros((toks, rows), F32)
        select = jnp.concatenate(
            [jnp.where(placed & is_token, one, none), jnp.where(placed & ~is_token, one, none)], axis=0
        ).astype(BF16)
        select_ref[...] = select
        done(loads[1:])
        table = table_ref[:, DIRECT:]
        out_ref[...] = lax.dot_general(
            select, table, (((0,), (0,)), ((), ())), preferred_element_type=F32
        ).astype(BF16)

    return call(
        kernel,
        [((rows, far), BF16), ((2 * toks, rows), BF16)],
        [pltpu.with_memory_space_constraint(v, pltpu.HBM) for v in (tokens, routes.T, cotangent)],
        [
            pltpu.VMEM((2 * toks, tokens.shape[1]), BF16),
            pltpu.VMEM((picks, toks), jnp.int32),
            pltpu.SemaphoreType.DMA((3,)),
        ],
        [HBM] * 3,
        4 * toks * rows * far,
        12,
    )


def partial_sums(plan, me, sources, sums, weights, limit):
    w = plan.width
    xs = [x for _, pieces in sources for x in pieces]
    rows = sum(x.shape[0] for x in sources[0][1])
    base = [] if sums is None else [sums]

    def kernel(me_ref, *refs):
        base_refs, x_refs = refs[: len(base)], list(refs[len(base) : len(base) + len(xs)])
        wg, wu, wd, out_ref = refs[len(base) + len(xs) : len(base) + len(xs) + 4]
        bufs, sems = refs[len(base) + len(xs) + 4 : -1], refs[-1]
        loads = [
            run(plan.copies(me_ref, k, DIRECT, plan.far, (wg, wu, wd), bufs[3 * i : 3 * i + 3], sems.at[i]))
            for i, (k, _) in enumerate(sources)
        ]
        for i, (_, pieces) in enumerate(sources):
            done(loads[i])
            first = 0
            for _ in pieces:
                x = x_refs.pop(0)
                last = first + x.shape[0]
                for t, term in enumerate(forward(x[...], bufs[3 * i : 3 * i + 3])):
                    cols = slice(t * w, (t + 1) * w)
                    if i > 0:
                        term = term + out_ref[first:last, cols]
                    elif base_refs:
                        term = term + base_refs[0][first:last, cols]
                    out_ref[first:last, cols] = term
                first = last

    return call(
        kernel,
        [((rows, 3 * w), F32)],
        (me, *base, *xs, *weights),
        plan.weight_scratch(plan.far) * len(sources) + [pltpu.SemaphoreType.DMA((len(sources), 3))],
        [SMEM] + [VMEM] * (len(base) + len(xs)) + [HBM] * 3,
        2 * rows * 3 * w * plan.far * len(sources),
        limit,
    )[0]


def gates(plan, me, sums, arrived, weights):
    rows, w = sums.shape[0], plan.width
    half, block = rows // 2, 128
    order = (2,)
    n = len(order)
    near_cols = plan.parts * DIRECT

    def kernel(me_ref, sums_hbm, *refs):
        x_hbm, (wg, wu, wd, out_ref, top_ref, bottom_ref, near_ref), rest = (
            refs[: 2 * n],
            refs[2 * n : 2 * n + 7],
            refs[2 * n + 7 :],
        )
        acc, x_buf, direct_buf = rest[:3]
        near, far, (n_sems, f_sems, x_sems, m_sems) = rest[3:6], rest[6:-4], rest[-4:]
        hbm = (wg, wu, wd)
        first_load = pltpu.make_async_copy(sums_hbm, acc, m_sems.at[0])
        first_load.start()
        loads = []
        for i, k in enumerate(order):
            weight_loads = run(plan.copies(me_ref, k, DIRECT, plan.far, hbm, far[3 * i : 3 * i + 3], f_sems.at[i]))
            x_loads = run(
                [pltpu.make_async_copy(x_hbm[2 * i + j], x_buf.at[2 * i + j], x_sems.at[2 * i + j]) for j in range(2)]
            )
            loads.append(weight_loads + x_loads)
        first_load.wait()
        done(loads[0][3:])
        for t in range(3):
            loads[0][t].wait()
            if t == 2:
                near_loads = [
                    c
                    for k in range(plan.parts)
                    for c in run(plan.copies(me_ref, k, 0, DIRECT, hbm, near, n_sems.at[k], k * DIRECT))
                ]
            for j in range(2):
                acc[j * half : (j + 1) * half, t * w : (t + 1) * w] += forward_one(x_buf[j], far, t)

        @pl.loop(0, rows // block)
        def _(b):
            r = pl.ds(pl.multiple_of(b * block, block), block)
            gate, up = acc[r, 0:w], acc[r, w : 2 * w]
            back = pltpu.roll(acc[r, 2 * w : 3 * w], block - CAP, 0)
            first = lax.broadcasted_iota(jnp.int32, (block, w), 0) % (2 * CAP) < CAP
            sig = jax.nn.sigmoid(gate)
            act = gate * sig
            zero = jnp.zeros_like(act)
            grad_gate = back * up * sig * (1.0 + gate * (1.0 - sig))
            grad_up = back * act
            out_ref[r, 0:w] = jnp.where(first, zero, pltpu.roll(grad_gate, CAP, 0)).astype(BF16)
            out_ref[r, w : 2 * w] = jnp.where(first, zero, pltpu.roll(grad_up, CAP, 0)).astype(BF16)
            out_ref[r, 2 * w : 3 * w] = jnp.where(first, act * up, zero).astype(BF16)

        done(near_loads)
        direct_buf[...] = backward(out_ref[...], near, w).astype(BF16)
        store = pltpu.make_async_copy(direct_buf, near_ref, m_sems.at[2])
        store.start()
        relay = backward(out_ref[...], far[-3:], w).astype(BF16)
        top_ref[...] = relay[:half]
        bottom_ref[...] = relay[half:]
        store.wait()

    scratch = [
        pltpu.VMEM((rows, 3 * w), F32),
        pltpu.VMEM((2 * n, half, plan.far), BF16),
        pltpu.VMEM((rows, near_cols), BF16),
        *plan.weight_scratch(near_cols),
        *(plan.weight_scratch(plan.far) * n),
        pltpu.SemaphoreType.DMA((plan.parts, 3)),
        pltpu.SemaphoreType.DMA((n, 3)),
        pltpu.SemaphoreType.DMA((2 * n,)),
        pltpu.SemaphoreType.DMA((3,)),
    ]
    out = call(
        kernel,
        [
            ((rows, 3 * w), BF16),
            ((half, plan.far), BF16),
            ((half, plan.far), BF16),
            ((rows, near_cols), BF16),
        ],
        (me, sums, *arrived, *weights),
        scratch,
        [SMEM] + [ANY] * (2 * n + 1) + [HBM] * 3,
        2 * rows * 3 * w * ((n + 1) * plan.far + near_cols),
        26,
        [VMEM, KEPT, KEPT, HBM],
    )
    return out


def near_sums(plan, me, sums, direct, weights):
    rows, w = sums.shape[0], plan.width
    near_cols = plan.parts * DIRECT

    def kernel(me_ref, sums_ref, x_hbm, wg, wu, wd, out_ref, x_ref, g, u, d, sems, x_sem):
        x_load = pltpu.make_async_copy(x_hbm, x_ref, x_sem.at[0])
        x_load.start()
        loads = [
            plan.copies(me_ref, k, 0, DIRECT, (wg, wu, wd), (g, u, d), sems.at[k], k * DIRECT)
            for k in range(plan.parts)
        ]
        by_matrix = [run([c[t] for c in loads]) for t in range(3)]
        x_load.wait()
        for t in range(3):
            done(by_matrix[t])
            c = slice(t * w, (t + 1) * w)
            out_ref[:, c] = sums_ref[:, c] + forward_one(x_ref[...], (g, u, d), t)

    return call(
        kernel,
        [((rows, 3 * w), F32)],
        (me, sums, direct, *weights),
        [pltpu.VMEM((rows, near_cols), BF16)]
        + plan.weight_scratch(near_cols)
        + [pltpu.SemaphoreType.DMA((plan.parts, 3)), pltpu.SemaphoreType.DMA((1,))],
        [SMEM, VMEM, ANY, HBM, HBM, HBM],
        2 * rows * 3 * w * near_cols,
        16,
    )[0]


def products(plan, me, h, wanted, weights):
    w = plan.width
    reach = plan.far
    adds = [a for *_, a in wanted if a is not None]
    outs = [((last - first, reach), BF16) for _, first, last, _ in wanted]

    def kernel(me_ref, h_ref, *refs):
        add_refs = list(refs[: len(adds)])
        wg, wu, wd = refs[len(adds) : len(adds) + 3]
        out_refs = refs[len(adds) + 3 : len(adds) + 3 + len(outs)]
        bufs, sems = refs[len(adds) + 3 + len(outs) : -1], refs[-1]
        loads = [
            run(plan.copies(me_ref, k, DIRECT, reach, (wg, wu, wd), bufs[3 * i : 3 * i + 3], sems.at[i]))
            for i, (k, *_) in enumerate(wanted)
        ]
        for i, (_, first, last, extra) in enumerate(wanted):
            done(loads[i])
            value = backward(h_ref[first:last, :], bufs[3 * i : 3 * i + 3], w)
            if extra is not None:
                value = value + add_refs.pop(0)[...].astype(F32)
            out_refs[i][...] = value.astype(BF16)

    return call(
        kernel,
        outs,
        (me, h, *adds, *weights),
        plan.weight_scratch(reach) * len(wanted) + [pltpu.SemaphoreType.DMA((len(wanted), 3))],
        [SMEM] + [VMEM] * (1 + len(adds)) + [HBM] * 3,
        sum(2 * (last - first) * 3 * w * reach for _, first, last, _ in wanted),
        16,
    )


def per_device(tokens, routes, combine, w_gate, w_up, w_down, cotangent):
    toks, _ = tokens.shape
    sources = lax.axis_size("expert")
    parts = lax.axis_size("hidden")
    group = 2 * CAP
    rows = sources * group
    half = rows // 2
    plan = Plan(parts, w_gate.shape[1], w_gate.shape[2])
    me = lax.axis_index("hidden").astype(jnp.int32).reshape(1)
    weights = tuple(
        pltpu.with_memory_space_constraint(w[0], pltpu.HBM) for w in (w_gate, w_up, w_down)
    )

    def shift(v, k):
        return lax.ppermute(v, "hidden", [(i, (i + k) % parts) for i in range(parts)])

    def exchange(v):
        out = lax.all_to_all(
            v.reshape(sources, group, v.shape[1]), "expert", split_axis=0, concat_axis=0, tiled=True
        )
        return out.reshape(rows, v.shape[1])

    direct = jnp.concatenate([tokens[:, :DIRECT], cotangent[:, :DIRECT]], axis=0)
    direct_parts = [direct] + [shift(direct, parts - k) for k in range(1, parts)]

    packed_far, select = pack_far(tokens, routes, cotangent, rows)

    def pack(values):
        return lax.dot_general(
            select, values, (((0,), (0,)), ((), ())), preferred_element_type=F32
        ).astype(BF16)

    own = exchange(packed_far)
    packed_direct = pack(jnp.concatenate(direct_parts, axis=1))
    own, packed_direct = lax.optimization_barrier((own, packed_direct))
    top, bottom = own[:half], own[half:]
    l_top = shift(top, 1)
    r_bottom = shift(bottom, -1)
    arrived_direct = exchange(packed_direct)
    l_bottom = shift(bottom, 1)
    r_top = shift(top, -1)
    o_top = shift(l_top, 1)
    o_bottom = shift(r_bottom, -1)
    sums = partial_sums(plan, me, [(0, [own])], None, weights, 14)
    sums = partial_sums(plan, me, [(3, [l_top, l_bottom]), (1, [r_top, r_bottom])], sums, weights, 18)
    sums = near_sums(plan, me, sums, arrived_direct, weights)
    grads, relay_top, relay_bottom, near = gates(plan, me, sums, (o_top, o_bottom), weights)

    o_top = shift(relay_top, 1)
    o_bottom = shift(relay_bottom, -1)
    back_direct = exchange(near)
    p_bottom, p_top = products(plan, me, grads, [(1, half, rows, None), (3, 0, half, None)], weights)
    l_bottom = shift(p_bottom, 1)
    r_top = shift(p_top, -1)
    p_top, p_bottom = products(plan, me, grads, [(1, 0, half, o_top), (3, half, rows, o_bottom)], weights)
    l_top = shift(p_top, 1)
    r_bottom = shift(p_bottom, -1)
    mine = products(plan, me, grads, [(0, 0, rows, None)], weights)[0]
    total = (
        mine.astype(F32)
        + jnp.concatenate([l_top, l_bottom], axis=0).astype(F32)
        + jnp.concatenate([r_top, r_bottom], axis=0).astype(F32)
    ).astype(BF16)
    total, back_direct = lax.optimization_barrier((total, back_direct))
    back_far = exchange(total)

    owner = lax.broadcasted_iota(jnp.int32, (toks, rows), 1) // group
    hit = routes[:, :, None] == owner[:, None, :]
    weight = jnp.sum(jnp.where(hit, combine[:, :, None], 0.0), axis=1)
    spread = select.astype(F32) * jnp.concatenate([weight, weight], axis=0)
    coarse = lax.reduce_precision(spread, 8, 7)
    fine = (spread - coarse).astype(BF16)
    coarse = coarse.astype(BF16)

    def mix(back):
        return dot(coarse, back) + dot(fine, back)

    mixed = mix(back_direct)
    near = mixed[:, :DIRECT]
    for k in range(1, parts):
        near = near + shift(mixed[:, k * DIRECT : (k + 1) * DIRECT].astype(BF16), k).astype(F32)
    result = jnp.concatenate([near.astype(BF16), mix(back_far).astype(BF16)], axis=1)
    return result[:toks], result[toks:]


def solution(mesh):
    return jax.shard_map(
        per_device,
        mesh=mesh,
        in_specs=(
            P("expert", "hidden"),
            P("expert", None),
            P("expert", None),
            P("expert", None, "hidden"),
            P("expert", None, "hidden"),
            P("expert", "hidden", None),
            P("expert", "hidden"),
        ),
        out_specs=(P("expert", "hidden"), P("expert", "hidden")),
        check_vma=False,
    )
```
